128 devices in a mesh: seq: 16 (over x_lo, y, core), head: 8 (over z, x_hi).
Axes of the slice: x: 4 (x_hi: 2, x_lo: 2; x = x_hi * 2 + x_lo), y: 4, z: 4, core: 2. Of those that a mesh axis runs over, the one named last changes fastest.
Arguments:
- queries: bfloat16 [16384, 4096], P('seq', 'head'), may hold values from -6 to 6
- key_states: bfloat16 [16384, 2048], P('seq', 'head'), may hold values from -6 to 6
- value_states: bfloat16 [16384, 2048], P('seq', 'head'), may hold values from -6 to 6
- outputs: bfloat16 [16384, 4096], P('seq', 'head'), may hold values from -6 to 6
- out_grad: bfloat16 [16384, 4096], P(('seq', 'head')), may hold values from -96 to 96
- log_norm: float32 [32, 16384], P('head', 'seq'), may hold values from 6 to 7.6
Outputs:
- query_grad: bfloat16 [16384, 4096], P(('seq', 'head'))
- key_grad: bfloat16 [16384, 2048], P(('seq', 'head'))
- value_grad: bfloat16 [16384, 2048], P(('seq', 'head'))
The draws below stay inside these ranges and needn't reach their ends.
All inputs are finite; a program needn't handle non-finite values.
Results may differ from the reference program's by a relative error of at most 0.0049.
Values may be sent and summed in bfloat16 or wider, within the bound.
No kernel may reach another device: no remote copies, remote signals or barrier semaphores. Data moves between devices by JAX's collectives and lax.ppermute only.
A program may use at most 128 MiB of HBM per device.

```python
import jax
import jax.numpy as jnp
from jax import lax

HEADS = 32
KV_HEADS = 16
HEAD_DIM = 128
WINDOW = 1024
LOCAL_TOK = 1024
SLAB = 16384


def block_scale(rng, shape, pieces, least, top_value):
    def one(axis_at, blocks):
        steps = jax.random.uniform(jax.random.fold_in(jax.random.fold_in(rng, 6), axis_at), (blocks,), jnp.float32, least / len(pieces), top_value / len(pieces))
        return jnp.repeat(jnp.exp(steps), shape[axis_at] // blocks).reshape((-1,) + (1,) * (len(shape) - axis_at - 1))

    level = one(*pieces[0])
    for cut in pieces[1:]:
        level = level * one(*cut)
    return level


def gaussian(rng, shape, scale, reach, pieces=(), held_as=jnp.bfloat16):
    drawn = scale * jax.random.normal(rng, shape, jnp.float32)
    if pieces:
        drawn = drawn * block_scale(rng, shape, pieces, -0.22, 0.18)
    return jnp.clip(drawn, -reach, reach).astype(held_as)


def setup_inputs(seed: int = 0) -> dict:
    arg_keys = jax.random.split(jax.random.key(seed), 7)
    queries = gaussian(arg_keys[0], (SLAB, HEADS * HEAD_DIM), 1.0, 6.0, ((0, 16), (1, 8)))
    key_states = gaussian(arg_keys[1], (SLAB, KV_HEADS * HEAD_DIM), 1.0, 6.0, ((0, 16), (1, 8)))
    value_states = gaussian(arg_keys[2], (SLAB, KV_HEADS * HEAD_DIM), 1.0, 6.0, ((0, 16), (1, 8)))
    outputs = gaussian(arg_keys[3], (SLAB, HEADS * HEAD_DIM), 1.0, 6.0, ((0, 16), (1, 8)))
    out_grad = gaussian(arg_keys[4], (SLAB, HEADS * HEAD_DIM), 16.0, 96.0, ((0, 128),))
    log_norm = jnp.clip(6.0 + 1.5999999 * jax.random.uniform(arg_keys[5], (HEADS, SLAB), jnp.float32) ** block_scale(arg_keys[5], (HEADS, SLAB), ((0, 8), (1, 16)), -0.2, 0.2), 6.0, 7.6)
    return dict(queries=queries, key_states=key_states, value_states=value_states, outputs=outputs, out_grad=out_grad, log_norm=log_norm)


score_scale = 168.0 ** -0.5


def reference(queries, key_states, value_states, outputs, out_grad, log_norm):
    seq_total = queries.shape[0]
    group_size = HEADS // KV_HEADS
    block_rows = min(512, LOCAL_TOK)
    block_count = seq_total // block_rows
    query_split = queries.reshape(seq_total, KV_HEADS, group_size, HEAD_DIM)
    grad_split = out_grad.reshape(seq_total, KV_HEADS, group_size, HEAD_DIM)
    grad_delta = jnp.sum(out_grad.astype(jnp.float32).reshape(seq_total, HEADS, HEAD_DIM) * outputs.astype(jnp.float32).reshape(seq_total, HEADS, HEAD_DIM), axis=2).T
    zeros_rim = jnp.zeros((WINDOW, KV_HEADS, HEAD_DIM), key_states.dtype)
    key_padded = jnp.concatenate([zeros_rim, key_states.reshape(seq_total, KV_HEADS, HEAD_DIM)], 0)
    value_padded = jnp.concatenate([zeros_rim, value_states.reshape(seq_total, KV_HEADS, HEAD_DIM)], 0)
    span_rows = WINDOW + block_rows

    def one_block(carried, block_index):
        grad_k_all, grad_v_all = carried
        row_start = block_index * block_rows
        q_rows = lax.dynamic_slice_in_dim(query_split, row_start, block_rows, 0).astype(jnp.float32)
        g_rows = lax.dynamic_slice_in_dim(grad_split, row_start, block_rows, 0).astype(jnp.float32)
        key_rows = lax.dynamic_slice_in_dim(key_padded, row_start, span_rows, 0).astype(jnp.float32)
        value_rows = lax.dynamic_slice_in_dim(value_padded, row_start, span_rows, 0).astype(jnp.float32)
        norm_rows = lax.dynamic_slice_in_dim(log_norm, row_start, block_rows, 1).reshape(KV_HEADS, group_size, block_rows)
        delta_rows = lax.dynamic_slice_in_dim(grad_delta, row_start, block_rows, 1).reshape(KV_HEADS, group_size, block_rows)
        scores = jnp.einsum("qhgd,khd->hgqk", q_rows, key_rows) * score_scale
        query_pos = row_start + jnp.arange(block_rows, dtype=jnp.int32)[:, None]
        key_pos = row_start - WINDOW + jnp.arange(span_rows, dtype=jnp.int32)[None, :]
        offset_gap = query_pos - key_pos
        allowed = (offset_gap >= 0) & (offset_gap < WINDOW) & (key_pos >= 0)
        probability = jnp.where(allowed, jnp.exp(scores - norm_rows[..., None]), 0.0)
        probs_low = lax.optimization_barrier(probability.astype(jnp.bfloat16)).astype(jnp.float32)
        grad_prob = jnp.einsum("qhgd,khd->hgqk", g_rows, value_rows)
        grad_score = lax.optimization_barrier((probability * (grad_prob - delta_rows[..., None])).astype(jnp.bfloat16)).astype(jnp.float32)
        grad_q = jnp.einsum("hgqk,khd->qhgd", grad_score, key_rows) * score_scale
        grad_k = jnp.einsum("hgqk,qhgd->khd", grad_score, q_rows) * score_scale
        grad_v = jnp.einsum("hgqk,qhgd->khd", probs_low, g_rows)
        old_k = lax.dynamic_slice_in_dim(grad_k_all, row_start, span_rows, 0)
        old_v = lax.dynamic_slice_in_dim(grad_v_all, row_start, span_rows, 0)
        grad_k_all = lax.dynamic_update_slice_in_dim(grad_k_all, old_k + grad_k, row_start, 0)
        grad_v_all = lax.dynamic_update_slice_in_dim(grad_v_all, old_v + grad_v, row_start, 0)
        return (grad_k_all, grad_v_all), grad_q.reshape(block_rows, HEADS * HEAD_DIM).astype(jnp.bfloat16)

    initial = (jnp.zeros((WINDOW + seq_total, KV_HEADS, HEAD_DIM), jnp.float32), jnp.zeros((WINDOW + seq_total, KV_HEADS, HEAD_DIM), jnp.float32))
    carried, grad_q_blocks = lax.scan(one_block, initial, jnp.arange(block_count, dtype=jnp.int32))
    grad_k_all, grad_v_all = carried
    query_grad = grad_q_blocks.reshape(seq_total, HEADS * HEAD_DIM)
    key_grad = grad_k_all[WINDOW:].reshape(seq_total, KV_HEADS * HEAD_DIM).astype(jnp.bfloat16)
    value_grad = grad_v_all[WINDOW:].reshape(seq_total, KV_HEADS * HEAD_DIM).astype(jnp.bfloat16)
    return (query_grad, key_grad, value_grad)
```

```python
import jax
import jax.numpy as jnp
from jax import lax
from jax.experimental import pallas as pl
from jax.experimental.pallas import tpu as pltpu
from jax.sharding import PartitionSpec as P

HEAD_DIM = 128
WINDOW = 1024
TOK = 1024
TILE = 256
PAIR = 2 * HEAD_DIM
SCALE = 168.0**-0.5
LOG2E = 1.4426950408889634
BIG = 1e30

ROWS_ROWS = (((1,), (1,)), ((), ()))
ROWS_COLS = (((1,), (0,)), ((), ()))
COLS_COLS = (((0,), (0,)), ((), ()))


def dot(a, b, dims):
    return lax.dot_general(a, b, dims, preferred_element_type=jnp.float32)


def band_kernel(
    edge_ref, q_ref, o_ref, g_ref, norm_ref, k_rim_ref, v_rim_ref, k_own_ref, v_own_ref,
    dq_ref, rim_ref, own_ref, keys, values, dk_sum, dv_sum, dq_sum, norm, delta,
):
    pair = pl.program_id(0)
    steps = TOK // TILE
    keys[0:TOK] = k_rim_ref[...]
    keys[TOK:] = k_own_ref[...]
    values[0:TOK] = v_rim_ref[...]
    values[TOK:] = v_own_ref[...]
    dk_sum[...] = jnp.zeros_like(dk_sum)
    dv_sum[...] = jnp.zeros_like(dv_sum)
    ones = jnp.ones((8, HEAD_DIM), jnp.bfloat16)
    for h in range(2):
        cols = slice(h * HEAD_DIM, (h + 1) * HEAD_DIM)
        terms = g_ref[:, cols].astype(jnp.float32) * o_ref[:, cols].astype(jnp.float32)
        high = terms.astype(jnp.bfloat16)
        low = (terms - high.astype(jnp.float32)).astype(jnp.bfloat16)
        delta[h] = dot(ones, high, ROWS_ROWS) + dot(ones, low, ROWS_ROWS)
        norm[h] = jnp.broadcast_to(norm_ref[pl.ds(pair * 2 + h, 1), :] * LOG2E, (8, TOK))
    rim_off = edge_ref[0]

    def tile(i, e, kind):
        at_q = pl.ds(pl.multiple_of(i * TILE, TILE), TILE)
        at_k = pl.ds(pl.multiple_of(e * TILE, TILE), TILE)
        k = keys[at_k, :]
        v = values[at_k, :]
        off = jnp.where(e * TILE < TOK, rim_off, 0.0)
        if kind:
            row = lax.broadcasted_iota(jnp.int32, (TILE, TILE), 0)
            col = lax.broadcasted_iota(jnp.int32, (TILE, TILE), 1)
            allowed = row > col if kind == 1 else row <= col
        probs = []
        grads = []
        for h in range(2):
            cols = slice(h * HEAD_DIM, (h + 1) * HEAD_DIM)
            scores = dot(k, q_ref[at_q, cols], ROWS_ROWS)
            prob = jnp.exp2(scores * (SCALE * LOG2E) - (norm[h, 0:1, at_q] + off))
            if kind:
                prob = jnp.where(allowed, prob, 0.0)
            grad_prob = dot(v, g_ref[at_q, cols], ROWS_ROWS)
            grads.append((prob * (grad_prob - delta[h, 0:1, at_q])).astype(jnp.bfloat16))
            probs.append(prob.astype(jnp.bfloat16))
        first, second = slice(0, HEAD_DIM), slice(HEAD_DIM, PAIR)
        dv_sum[at_k, :] += dot(probs[0], g_ref[at_q, first], ROWS_COLS) + dot(
            probs[1], g_ref[at_q, second], ROWS_COLS
        )
        dk_sum[at_k, :] += dot(grads[0], q_ref[at_q, first], ROWS_COLS) + dot(
            grads[1], q_ref[at_q, second], ROWS_COLS
        )
        for h in range(2):
            dq_sum[h] += dot(k, grads[h], COLS_COLS)

    def query_tile(i, carried):
        dq_sum[...] = jnp.zeros_like(dq_sum)
        tile(i, i, 1)
        for a in range(1, steps):
            tile(i, i + a, 0)
        tile(i, i + steps, 2)
        at_q = pl.ds(pl.multiple_of(i * TILE, TILE), TILE)
        for h in range(2):
            cols = slice(h * HEAD_DIM, (h + 1) * HEAD_DIM)
            dq_ref[at_q, cols] = (dq_sum[h] * SCALE).T.astype(jnp.bfloat16)
        return carried

    lax.fori_loop(0, steps, query_tile, 0)
    rim_ref[:, 0:HEAD_DIM] = (dk_sum[0:TOK] * SCALE).astype(jnp.bfloat16)
    rim_ref[:, HEAD_DIM:] = dv_sum[0:TOK].astype(jnp.bfloat16)
    own_ref[:, 0:HEAD_DIM] = dk_sum[TOK:] * SCALE
    own_ref[:, HEAD_DIM:] = dv_sum[TOK:]


def band(edge, q, o, g, norm, k_rim, v_rim, k_own, v_own):
    wide = pl.BlockSpec((TOK, PAIR), lambda i: (0, i))
    narrow = pl.BlockSpec((TOK, HEAD_DIM), lambda i: (0, i))
    shape = jax.ShapeDtypeStruct
    return pl.pallas_call(
        band_kernel,
        grid=(2,),
        in_specs=[
            pl.BlockSpec(memory_space=pltpu.SMEM), wide, wide, wide,
            pl.BlockSpec((4, TOK), lambda i: (0, 0)), narrow, narrow, narrow, narrow,
        ],
        out_specs=[wide, wide, wide],
        out_shape=[
            shape((TOK, 2 * PAIR), jnp.bfloat16),
            shape((TOK, 2 * PAIR), jnp.bfloat16),
            shape((TOK, 2 * PAIR), jnp.float32),
        ],
        scratch_shapes=[
            pltpu.VMEM((2 * TOK, HEAD_DIM), jnp.bfloat16),
            pltpu.VMEM((2 * TOK, HEAD_DIM), jnp.bfloat16),
            pltpu.VMEM((2 * TOK, HEAD_DIM), jnp.float32),
            pltpu.VMEM((2 * TOK, HEAD_DIM), jnp.float32),
            pltpu.VMEM((2, HEAD_DIM, TILE), jnp.float32),
            pltpu.VMEM((2, 8, TOK), jnp.float32),
            pltpu.VMEM((2, 8, TOK), jnp.float32),
        ],
        compiler_params=pltpu.CompilerParams(vmem_limit_bytes=40 * 1024 * 1024),
        cost_estimate=pl.CostEstimate(
            flops=8 * 10**9, bytes_accessed=10 * 2**20, transcendentals=5 * 10**6
        ),
    )(edge, q, o, g, norm, k_rim, v_rim, k_own, v_own)


def from_behind(shard, by):
    devices = lax.axis_size("seq")
    pairs = [(i, i + by) for i in range(devices) if 0 <= i + by < devices]
    return lax.ppermute(shard, "seq", pairs)


def to_heads(x):
    members = lax.axis_size("head")
    rows, width = x.shape
    parts = x.reshape(rows, members, width // members).transpose(1, 0, 2)
    parts = lax.all_to_all(parts, "head", split_axis=0, concat_axis=0, tiled=True)
    return parts.reshape(members * rows, width // members)


def to_tokens(x):
    members = lax.axis_size("head")
    parts = x.reshape(members, x.shape[0] // members, x.shape[1])
    return lax.all_to_all(parts, "head", split_axis=0, concat_axis=0, tiled=True)


def on_device(queries, key_states, value_states, outputs, out_grad, log_norm):
    k_rim = from_behind(key_states, 1)
    v_rim = from_behind(value_states, 1)
    grad_local = to_heads(out_grad)
    edge = jnp.where(lax.axis_index("seq") == 0, BIG, 0.0).astype(jnp.float32).reshape(1)
    dq, rim, own = band(
        edge, queries, outputs, grad_local, log_norm, k_rim, v_rim, key_states, value_states
    )
    later = from_behind(rim, -1)
    dkv = (own + later.astype(jnp.float32)).astype(jnp.bfloat16)
    dq = to_tokens(dq)
    dkv = to_tokens(dkv)
    members, rows, width = dq.shape
    dq = dq.transpose(1, 0, 2).reshape(rows, members * width)
    dkv = dkv.reshape(members, rows, 2, 2, HEAD_DIM).transpose(3, 1, 0, 2, 4)
    dkv = dkv.reshape(2, rows, members * PAIR)
    return dq, dkv[0], dkv[1]


def solution(mesh):
    placed = (
        P("seq", "head"),
        P("seq", "head"),
        P("seq", "head"),
        P("seq", "head"),
        P(("seq", "head"), None),
        P("head", "seq"),
    )
    return jax.shard_map(
        on_device,
        mesh=mesh,
        in_specs=placed,
        out_specs=(P(("seq", "head"), None), P(("seq", "head"), None), P(("seq", "head"), None)),
        check_vma=False,
    )
```

```python
import functools

import jax
import jax.numpy as jnp
from jax import lax
from jax.experimental import pallas as pl
from jax.experimental.pallas import tpu as pltpu
from jax.sharding import PartitionSpec as P


HEAD_DIM = 128
TOK = 1024
TILE = 256
PAIR = 2 * HEAD_DIM
SCALE = 168.0**-0.5
LOG2E = 1.4426950408889634
BIG = 1e30

ROWS_ROWS = (((1,), (1,)), ((), ()))
ROWS_COLS = (((1,), (0,)), ((), ()))
COLS_COLS = (((0,), (0,)), ((), ()))


def dot(a, b, dims):
    return lax.dot_general(a, b, dims, preferred_element_type=jnp.float32)


HEADS = [slice(h * HEAD_DIM, (h + 1) * HEAD_DIM) for h in range(2)]
STEPS = TOK // TILE


def band_kernel(own, *refs):
    if own:
        norm_ref, q_ref, g_ref, delta_ref, k_ref, v_ref, part_ref, dq_ref, dkv_ref = refs[:9]
    else:
        edge_ref, norm_ref, *refs = refs
        q_ref, g_ref, o_ref, k_ref, va_ref, *vb_refs = refs[:7]
        part_ref, dkv_ref, delta_ref, v_ref = refs[7:11]
    norm, dk_sum, dv_sum = refs[-3:]
    pair = pl.program_id(0)
    for h in range(2):
        row = norm_ref[pl.ds(pair * 2 + h, 1), :] * LOG2E
        if not own:
            row = row + edge_ref[0]
        norm[h] = jnp.broadcast_to(row, (8, TOK))

    if not own:
        for n, vb_ref in enumerate(vb_refs):
            at = slice(n * TOK // 2, (n + 1) * TOK // 2)
            v_ref[at, :] = va_ref[at, :] + vb_ref[...]
        ones = jnp.ones((8, HEAD_DIM), jnp.bfloat16)
        for h in range(2):
            terms = g_ref[:, HEADS[h]].astype(jnp.float32) * o_ref[:, HEADS[h]].astype(jnp.float32)
            high = terms.astype(jnp.bfloat16)
            low = (terms - high.astype(jnp.float32)).astype(jnp.bfloat16)
            total = dot(ones, high, ROWS_ROWS) + dot(ones, low, ROWS_ROWS)
            delta_ref[8 * h : 8 * h + 8, :] = total

    def tile(i, e, dq):
        at_q = slice(i * TILE, (i + 1) * TILE)
        at_k = slice(e * TILE, (e + 1) * TILE)
        k = k_ref[at_k, :]
        v = v_ref[at_k, :]
        if i == e:
            row = lax.broadcasted_iota(jnp.int32, (TILE, TILE), 0)
            col = lax.broadcasted_iota(jnp.int32, (TILE, TILE), 1)
            allowed = row <= col if own else row > col
        probs = []
        grads = []
        for h in range(2):
            scores = dot(k, q_ref[at_q, HEADS[h]], ROWS_ROWS)
            prob = jnp.exp2(scores * (SCALE * LOG2E) - norm[h, 0:1, at_q])
            if i == e:
                prob = jnp.where(allowed, prob, 0.0)
            grad_prob = dot(v, g_ref[at_q, HEADS[h]], ROWS_ROWS)
            delta = delta_ref[8 * h : 8 * h + 1, at_q]
            grads.append((prob * (grad_prob - delta)).astype(jnp.bfloat16))
            probs.append(prob.astype(jnp.bfloat16))
        dv = dot(probs[0], g_ref[at_q, HEADS[0]], ROWS_COLS) + dot(
            probs[1], g_ref[at_q, HEADS[1]], ROWS_COLS
        )
        dk = dot(grads[0], q_ref[at_q, HEADS[0]], ROWS_COLS) + dot(
            grads[1], q_ref[at_q, HEADS[1]], ROWS_COLS
        )
        if i == (e if own else 0):
            dv_sum[at_k, :] = dv
            dk_sum[at_k, :] = dk
        else:
            dv_sum[at_k, :] += dv
            dk_sum[at_k, :] += dk
        return [d + dot(k, grads[h], COLS_COLS) for h, d in enumerate(dq)]

    for i in range(STEPS):
        at_q = slice(i * TILE, (i + 1) * TILE)
        if own:
            dq = [part_ref[rows, at_q] for rows in HEADS]
        else:
            dq = [jnp.zeros((HEAD_DIM, TILE), jnp.float32)] * 2
        for e in range(0, i + 1) if own else range(i, STEPS):
            dq = tile(i, e, dq)
        for h in range(2):
            if own:
                dq_ref[at_q, HEADS[h]] = (dq[h] * SCALE).T.astype(jnp.bfloat16)
            else:
                part_ref[HEADS[h], at_q] = dq[h]
    kind = dkv_ref.dtype
    dkv_ref[:, 0:HEAD_DIM] = (dk_sum[...] * SCALE).astype(kind)
    dkv_ref[:, HEAD_DIM:] = dv_sum[...].astype(kind)


def band(own, *operands):
    spec = pl.BlockSpec
    wide = spec((TOK, PAIR), lambda i: (0, i))
    tall = spec((PAIR, TOK), lambda i: (i, 0))
    narrow = spec((TOK, HEAD_DIM), lambda i: (0, i))
    lines = spec((16, TOK), lambda i: (i, 0))
    shape = jax.ShapeDtypeStruct
    norm = spec((4, TOK), lambda i: (0, 0))
    scratch = [
        pltpu.VMEM((2, 8, TOK), jnp.float32),
        pltpu.VMEM((TOK, HEAD_DIM), jnp.float32),
        pltpu.VMEM((TOK, HEAD_DIM), jnp.float32),
    ]
    if own:
        in_specs = [norm, wide, wide, lines, narrow, narrow, tall]
        out_specs = [wide, wide]
        out_shape = [
            pltpu.HBM((TOK, 2 * PAIR), jnp.bfloat16),
            shape((TOK, 2 * PAIR), jnp.float32),
        ]
    else:
        half = spec((TOK // 2, HEAD_DIM), lambda i: (0, i))
        in_specs = [spec(memory_space=pltpu.SMEM), norm, wide, wide, wide, narrow, narrow, half, half]
        out_specs = [tall, wide, lines]
        out_shape = [
            shape((2 * PAIR, TOK), jnp.float32),
            shape((TOK, 2 * PAIR), jnp.bfloat16),
            shape((32, TOK), jnp.float32),
        ]
        scratch = [pltpu.VMEM((TOK, HEAD_DIM), jnp.bfloat16)] + scratch
    return pl.pallas_call(
        functools.partial(band_kernel, own),
        name="own_band" if own else "rim_band",
        grid=(2,),
        in_specs=in_specs,
        out_specs=out_specs,
        out_shape=out_shape,
        scratch_shapes=scratch,
        compiler_params=pltpu.CompilerParams(vmem_limit_bytes=24000 * 1024),
        cost_estimate=pl.CostEstimate(
            flops=4 * 10**9, bytes_accessed=8 * 2**20, transcendentals=3 * 10**6
        ),
    )(*operands)


def from_behind(shard, by, skip=None):
    devices = lax.axis_size("seq")
    pairs = [(i, i + by) for i in range(devices) if 0 <= i + by < devices and i != skip]
    return lax.ppermute(shard, "seq", pairs)


def prepare_kernel(g_ref, parts_ref, sem):
    members, _, width = parts_ref.shape
    copies = [
        pltpu.make_async_copy(g_ref.at[:, pl.ds(i * width, width)], parts_ref.at[i], sem.at[i])
        for i in range(members)
    ]
    for copy in copies:
        copy.start()
    for copy in copies:
        copy.wait()


def prepare(out_grad):
    members = lax.axis_size("head")
    rows, width = out_grad.shape
    shape = (members, rows, width // members)
    return pl.pallas_call(
        prepare_kernel,
        name="prepare",
        grid=(1,),
        in_specs=[pl.BlockSpec(memory_space=pl.ANY)],
        out_specs=pl.BlockSpec(shape, lambda i: (0, 0, 0)),
        out_shape=jax.ShapeDtypeStruct(shape, out_grad.dtype),
        scratch_shapes=[pltpu.SemaphoreType.DMA((members,))],
        compiler_params=pltpu.CompilerParams(vmem_limit_bytes=60 * 1024 * 1024),
        cost_estimate=pl.CostEstimate(flops=0, bytes_accessed=2 * 2**20, transcendentals=0),
    )(out_grad)


HOPS = [(0, 0), (1, 0), (0, 1), (3, 0), (2, 1), (2, 0), (1, 1), (3, 1)]


def sum_kernel(me_ref, own_ref, later_ref, *out_refs):
    rows = out_refs[0].shape[0]
    for hop, out_ref in zip(HOPS, out_refs):
        at = pl.ds(pl.multiple_of(partner(me_ref[0], hop) * rows, rows), rows)
        total = own_ref[at, :] + later_ref[at, :].astype(jnp.float32)
        out_ref[...] = total.astype(out_ref.dtype)


def sum_parts(me, own, later):
    members = lax.axis_size("head")
    rows = TOK // members
    vmem = pl.BlockSpec(memory_space=pltpu.VMEM)
    return pl.pallas_call(
        sum_kernel,
        name="sum_parts",
        in_specs=[pl.BlockSpec(memory_space=pltpu.SMEM), vmem, vmem],
        out_specs=[vmem] * members,
        out_shape=[jax.ShapeDtypeStruct((rows, 2 * PAIR), jnp.bfloat16)] * members,
        compiler_params=pltpu.CompilerParams(vmem_limit_bytes=16 * 2**20),
        cost_estimate=pl.CostEstimate(flops=10**6, bytes_accessed=4 * 2**20, transcendentals=0),
    )(me, own, later)


def join_kernel(me_ref, *refs):
    *in_refs, key_ref, value_ref = refs
    for shift, in_ref in enumerate(in_refs):
        source = partner(me_ref[0], (4 - HOPS[shift][0], HOPS[shift][1]))
        for g in range(2):
            to = pl.ds(pl.multiple_of(source * PAIR + g * HEAD_DIM, HEAD_DIM), HEAD_DIM)
            key_ref[:, to] = in_ref[:, g * PAIR : g * PAIR + HEAD_DIM]
            value_ref[:, to] = in_ref[:, g * PAIR + HEAD_DIM : (g + 1) * PAIR]


def join(me, parts):
    members = len(parts)
    rows = parts[0].shape[0]
    vmem = pl.BlockSpec(memory_space=pltpu.VMEM)
    out = jax.ShapeDtypeStruct((rows, members * PAIR), parts[0].dtype)
    return pl.pallas_call(
        join_kernel,
        name="join",
        grid=(1,),
        in_specs=[pl.BlockSpec(memory_space=pltpu.SMEM)]
        + [pl.BlockSpec(parts[0].shape, lambda i: (0, 0))] * members,
        out_specs=[pl.BlockSpec(out.shape, lambda i: (0, 0))] * 2,
        out_shape=[out, out],
        compiler_params=pltpu.CompilerParams(vmem_limit_bytes=16 * 2**20),
        cost_estimate=pl.CostEstimate(flops=0, bytes_accessed=4 * 2**20, transcendentals=0),
    )(me, *parts)


def exchange(parts):
    return lax.all_to_all(parts, "head", split_axis=0, concat_axis=0, tiled=True)


def partner(i, hop):
    z, half = hop
    return (i + 2 * z) % 8 ^ half


def shift_heads(x, hop):
    return lax.ppermute(x, "head", [(i, partner(i, hop)) for i in range(8)])


def on_device(queries, key_states, value_states, outputs, out_grad, log_norm):
    members = lax.axis_size("head")
    me = lax.axis_index("head").astype(jnp.int32).reshape(1)
    edge = jnp.where(lax.axis_index("seq") == 0, BIG, 0.0).astype(jnp.float32).reshape(1)
    half = lax.axis_size("seq") // 2
    middle = (1, half - 3)
    detours = []
    for n in range(2):
        rows = value_states[n * TOK // 2 : (n + 1) * TOK // 2]
        detours.append(lax.ppermute(rows, "seq", [(half - 1, middle[n])]))
    k_rim = from_behind(key_states, 1)
    v_rim = from_behind(value_states, 1, skip=half - 1)
    grad_parts = prepare(out_grad)
    grad_local = exchange(grad_parts).reshape(TOK, 2 * PAIR)
    v_far = []
    for n in range(2):
        v_far.append(lax.ppermute(detours[n], "seq", [(middle[n], half)]))
    queries = pltpu.with_memory_space_constraint(queries, pltpu.HBM)
    part, rim, delta = band(
        False, edge, log_norm, queries, grad_local, outputs, k_rim, v_rim, *v_far
    )
    later = from_behind(rim, -1)
    dq, own = band(True, log_norm, queries, grad_local, delta, key_states, value_states, part)
    dq = exchange(dq.reshape(members, TOK // members, 2 * PAIR))
    dkv = sum_parts(me, own, later)
    dkv = [dkv[0]] + [shift_heads(x, hop) for x, hop in zip(dkv[1:], HOPS[1:])]
    key_grad, value_grad = join(me, dkv)
    dq = dq.transpose(1, 0, 2).reshape(TOK // members, members * 2 * PAIR)
    return dq, key_grad, value_grad


def solution(mesh):
    placed = (
        P("seq", "head"),
        P("seq", "head"),
        P("seq", "head"),
        P("seq", "head"),
        P(("seq", "head"), None),
        P("head", "seq"),
    )
    return jax.shard_map(
        on_device,
        mesh=mesh,
        in_specs=placed,
        out_specs=(P(("seq", "head"), None), P(("seq", "head"), None), P(("seq", "head"), None)),
        check_vma=False,
    )
```

```python
import functools

import jax
import jax.numpy as jnp
from jax import lax
from jax.experimental import pallas as pl
from jax.experimental.pallas import tpu as pltpu
from jax.sharding import PartitionSpec as P


HEAD_DIM = 128
TOK = 1024
TILE = 256
PAIR = 2 * HEAD_DIM
SCALE = 168.0**-0.5
LOG2E = 1.4426950408889634
BIG = 1e30

ROWS_ROWS = (((1,), (1,)), ((), ()))
ROWS_COLS = (((1,), (0,)), ((), ()))
COLS_COLS = (((0,), (0,)), ((), ()))


def dot(a, b, dims):
    return lax.dot_general(a, b, dims, preferred_element_type=jnp.float32)


HEADS = [slice(h * HEAD_DIM, (h + 1) * HEAD_DIM) for h in range(2)]
STEPS = TOK // TILE


def band_kernel(own, *refs):
    if own:
        norm_ref, q_ref, g_ref, delta_ref, k_ref, v_ref, part_ref, dq_ref, dkv_ref = refs[:9]
    else:
        edge_ref, norm_ref, *refs = refs
        q_ref, g_ref, o_ref, k_ref, va_ref, *vb_refs = refs[:7]
        part_ref, dkv_ref, delta_ref, v_ref = refs[7:11]
    norm, dk_sum, dv_sum = refs[-3:]
    pair = pl.program_id(0)
    for h in range(2):
        row = norm_ref[pl.ds(pair * 2 + h, 1), :] * LOG2E
        if not own:
            row = row + edge_ref[0]
        norm[h] = jnp.broadcast_to(row, (8, TOK))

    if not own:
        for n, vb_ref in enumerate(vb_refs):
            at = slice(n * TOK // 2, (n + 1) * TOK // 2)
            v_ref[at, :] = va_ref[at, :] + vb_ref[...]
        ones = jnp.ones((8, HEAD_DIM), jnp.bfloat16)
        for h in range(2):
            terms = g_ref[:, HEADS[h]].astype(jnp.float32) * o_ref[:, HEADS[h]].astype(jnp.float32)
            high = terms.astype(jnp.bfloat16)
            low = (terms - high.astype(jnp.float32)).astype(jnp.bfloat16)
            total = dot(ones, high, ROWS_ROWS) + dot(ones, low, ROWS_ROWS)
            delta_ref[8 * h : 8 * h + 8, :] = total

    def tile(i, e, dq):
        at_q = slice(i * TILE, (i + 1) * TILE)
        at_k = slice(e * TILE, (e + 1) * TILE)
        k = k_ref[at_k, :]
        v = v_ref[at_k, :]
        if i == e:
            row = lax.broadcasted_iota(jnp.int32, (TILE, TILE), 0)
            col = lax.broadcasted_iota(jnp.int32, (TILE, TILE), 1)
            allowed = row <= col if own else row > col
        probs = []
        grads = []
        for h in range(2):
            scores = dot(k, q_ref[at_q, HEADS[h]], ROWS_ROWS)
            prob = jnp.exp2(scores * (SCALE * LOG2E) - norm[h, 0:1, at_q])
            if i == e:
                prob = jnp.where(allowed, prob, 0.0)
            grad_prob = dot(v, g_ref[at_q, HEADS[h]], ROWS_ROWS)
            delta = delta_ref[8 * h : 8 * h + 1, at_q]
            grads.append((prob * (grad_prob - delta)).astype(jnp.bfloat16))
            probs.append(prob.astype(jnp.bfloat16))
        dv = dot(probs[0], g_ref[at_q, HEADS[0]], ROWS_COLS) + dot(
            probs[1], g_ref[at_q, HEADS[1]], ROWS_COLS
        )
        dk = dot(grads[0], q_ref[at_q, HEADS[0]], ROWS_COLS) + dot(
            grads[1], q_ref[at_q, HEADS[1]], ROWS_COLS
        )
        if i == (e if own else 0):
            dv_sum[at_k, :] = dv
            dk_sum[at_k, :] = dk
        else:
            dv_sum[at_k, :] += dv
            dk_sum[at_k, :] += dk
        return [d + dot(k, grads[h], COLS_COLS) for h, d in enumerate(dq)]

    for i in range(STEPS):
        at_q = slice(i * TILE, (i + 1) * TILE)
        if own:
            dq = [part_ref[rows, at_q] for rows in HEADS]
        else:
            dq = [jnp.zeros((HEAD_DIM, TILE), jnp.float32)] * 2
        for e in range(0, i + 1) if own else range(i, STEPS):
            dq = tile(i, e, dq)
        for h in range(2):
            if own:
                dq_ref[at_q, HEADS[h]] = (dq[h] * SCALE).T.astype(jnp.bfloat16)
            else:
                part_ref[HEADS[h], at_q] = dq[h]
    kind = dkv_ref.dtype
    dkv_ref[:, 0:HEAD_DIM] = (dk_sum[...] * SCALE).astype(kind)
    dkv_ref[:, HEAD_DIM:] = dv_sum[...].astype(kind)


def band(own, *operands):
    spec = pl.BlockSpec
    wide = spec((TOK, PAIR), lambda i: (0, i))
    tall = spec((PAIR, TOK), lambda i: (i, 0))
    narrow = spec((TOK, HEAD_DIM), lambda i: (0, i))
    lines = spec((16, TOK), lambda i: (i, 0))
    shape = jax.ShapeDtypeStruct
    norm = spec((4, TOK), lambda i: (0, 0))
    scratch = [
        pltpu.VMEM((2, 8, TOK), jnp.float32),
        pltpu.VMEM((TOK, HEAD_DIM), jnp.float32),
        pltpu.VMEM((TOK, HEAD_DIM), jnp.float32),
    ]
    if own:
        in_specs = [norm, wide, wide, lines, narrow, narrow, tall]
        out_specs = [wide, wide]
        out_shape = [
            pltpu.HBM((TOK, 2 * PAIR), jnp.bfloat16),
            shape((TOK, 2 * PAIR), jnp.float32),
        ]
    else:
        half = spec((TOK // 2, HEAD_DIM), lambda i: (0, i))
        in_specs = [spec(memory_space=pltpu.SMEM), norm, wide, wide, wide, narrow, narrow, half, half]
        out_specs = [tall, wide, lines]
        out_shape = [
            shape((2 * PAIR, TOK), jnp.float32),
            shape((TOK, 2 * PAIR), jnp.bfloat16),
            shape((32, TOK), jnp.float32),
        ]
        scratch = [pltpu.VMEM((TOK, HEAD_DIM), jnp.bfloat16)] + scratch
    return pl.pallas_call(
        functools.partial(band_kernel, own),
        name="own_band" if own else "rim_band",
        grid=(2,),
        in_specs=in_specs,
        out_specs=out_specs,
        out_shape=out_shape,
        scratch_shapes=scratch,
        compiler_params=pltpu.CompilerParams(vmem_limit_bytes=24000 * 1024),
        cost_estimate=pl.CostEstimate(
            flops=4 * 10**9, bytes_accessed=8 * 2**20, transcendentals=3 * 10**6
        ),
    )(*operands)


def from_behind(shard, by, skip=None):
    devices = lax.axis_size("seq")
    pairs = [(i, i + by) for i in range(devices) if 0 <= i + by < devices and i != skip]
    return lax.ppermute(shard, "seq", pairs)


def prepare_kernel(g_ref, parts_ref, sem):
    members, _, width = parts_ref.shape
    copies = [
        pltpu.make_async_copy(g_ref.at[:, pl.ds(i * width, width)], parts_ref.at[i], sem.at[i])
        for i in range(members)
    ]
    for copy in copies:
        copy.start()
    for copy in copies:
        copy.wait()


def prepare(out_grad):
    members = lax.axis_size("head")
    rows, width = out_grad.shape
    shape = (members, rows, width // members)
    return pl.pallas_call(
        prepare_kernel,
        name="prepare",
        grid=(1,),
        in_specs=[pl.BlockSpec(memory_space=pl.ANY)],
        out_specs=pl.BlockSpec(shape, lambda i: (0, 0, 0)),
        out_shape=jax.ShapeDtypeStruct(shape, out_grad.dtype),
        scratch_shapes=[pltpu.SemaphoreType.DMA((members,))],
        compiler_params=pltpu.CompilerParams(vmem_limit_bytes=60 * 1024 * 1024),
        cost_estimate=pl.CostEstimate(flops=0, bytes_accessed=2 * 2**20, transcendentals=0),
    )(out_grad)


HOPS = [(0, 0), (1, 0), (0, 1), (3, 0), (2, 1), (2, 0), (1, 1), (3, 1)]


def sum_kernel(me_ref, own_ref, later_ref, *out_refs):
    rows = out_refs[0].shape[0]
    for hop, out_ref in zip(HOPS, out_refs):
        at = pl.ds(pl.multiple_of(partner(me_ref[0], hop) * rows, rows), rows)
        total = own_ref[at, :] + later_ref[at, :].astype(jnp.float32)
        out_ref[...] = total.astype(out_ref.dtype)


def sum_parts(me, own, later):
    members = lax.axis_size("head")
    rows = TOK // members
    vmem = pl.BlockSpec(memory_space=pltpu.VMEM)
    return pl.pallas_call(
        sum_kernel,
        name="sum_parts",
        in_specs=[pl.BlockSpec(memory_space=pltpu.SMEM), vmem, vmem],
        out_specs=[vmem] * members,
        out_shape=[jax.ShapeDtypeStruct((rows, 2 * PAIR), jnp.bfloat16)] * members,
        compiler_params=pltpu.CompilerParams(vmem_limit_bytes=16 * 2**20),
        cost_estimate=pl.CostEstimate(flops=10**6, bytes_accessed=4 * 2**20, transcendentals=0),
    )(me, own, later)


def join_kernel(me_ref, *refs):
    *in_refs, key_ref, value_ref = refs
    for shift, in_ref in enumerate(in_refs):
        source = partner(me_ref[0], (4 - HOPS[shift][0], HOPS[shift][1]))
        for g in range(2):
            to = pl.ds(pl.multiple_of(source * PAIR + g * HEAD_DIM, HEAD_DIM), HEAD_DIM)
            key_ref[:, to] = in_ref[:, g * PAIR : g * PAIR + HEAD_DIM]
            value_ref[:, to] = in_ref[:, g * PAIR + HEAD_DIM : (g + 1) * PAIR]


def join(me, parts):
    members = len(parts)
    rows = parts[0].shape[0]
    vmem = pl.BlockSpec(memory_space=pltpu.VMEM)
    out = jax.ShapeDtypeStruct((rows, members * PAIR), parts[0].dtype)
    return pl.pallas_call(
        join_kernel,
        name="join",
        grid=(1,),
        in_specs=[pl.BlockSpec(memory_space=pltpu.SMEM)]
        + [pl.BlockSpec(parts[0].shape, lambda i: (0, 0))] * members,
        out_specs=[pl.BlockSpec(out.shape, lambda i: (0, 0))] * 2,
        out_shape=[out, out],
        compiler_params=pltpu.CompilerParams(vmem_limit_bytes=16 * 2**20),
        cost_estimate=pl.CostEstimate(flops=0, bytes_accessed=4 * 2**20, transcendentals=0),
    )(me, *parts)


def exchange(parts):
    return lax.all_to_all(parts, "head", split_axis=0, concat_axis=0, tiled=True)


def partner(i, hop):
    z, half = hop
    return (i + 2 * z) % 8 ^ half


def shift_heads(x, hop):
    return lax.ppermute(x, "head", [(i, partner(i, hop)) for i in range(8)])


def on_device(queries, key_states, value_states, outputs, out_grad, log_norm):
    members = lax.axis_size("head")
    me = lax.axis_index("head").astype(jnp.int32).reshape(1)
    edge = jnp.where(lax.axis_index("seq") == 0, BIG, 0.0).astype(jnp.float32).reshape(1)
    half = lax.axis_size("seq") // 2
    middle = (1, half - 5)
    detours = []
    for n in range(2):
        rows = value_states[n * TOK // 2 : (n + 1) * TOK // 2]
        detours.append(lax.ppermute(rows, "seq", [(half - 1, middle[n])]))
    k_rim = from_behind(key_states, 1)
    v_rim = from_behind(value_states, 1, skip=half - 1)
    grad_parts = prepare(out_grad)
    grad_local = exchange(grad_parts).reshape(TOK, 2 * PAIR)
    v_far = []
    for n in range(2):
        v_far.append(lax.ppermute(detours[n], "seq", [(middle[n], half)]))
    queries_rim = pltpu.with_memory_space_constraint(queries, pltpu.HBM)
    part, rim, delta = band(
        False, edge, log_norm, queries_rim, grad_local, outputs, k_rim, v_rim, *v_far
    )
    later = from_behind(rim, -1)
    dq, own = band(True, log_norm, queries, grad_local, delta, key_states, value_states, part)
    dq = exchange(dq.reshape(members, TOK // members, 2 * PAIR))
    dkv = sum_parts(me, own, later)
    dkv = [dkv[0]] + [shift_heads(x, hop) for x, hop in zip(dkv[1:], HOPS[1:])]
    key_grad, value_grad = join(me, dkv)
    dq = dq.transpose(1, 0, 2).reshape(TOK // members, members * 2 * PAIR)
    return dq, key_grad, value_grad


def solution(mesh):
    placed = (
        P("seq", "head"),
        P("seq", "head"),
        P("seq", "head"),
        P("seq", "head"),
        P(("seq", "head"), None),
        P("head", "seq"),
    )
    return jax.shard_map(
        on_device,
        mesh=mesh,
        in_specs=placed,
        out_specs=(P(("seq", "head"), None), P(("seq", "head"), None), P(("seq", "head"), None)),
        check_vma=False,
    )
```

```python
import functools

import jax
import jax.numpy as jnp
from jax import lax
from jax.experimental import pallas as pl
from jax.experimental.pallas import tpu as pltpu
from jax.sharding import PartitionSpec as P


HEAD_DIM = 128
TOK = 1024
TILE = 256
PAIR = 2 * HEAD_DIM
SCALE = 168.0**-0.5
LOG2E = 1.4426950408889634
BIG = 1e30

ROWS_ROWS = (((1,), (1,)), ((), ()))
ROWS_COLS = (((1,), (0,)), ((), ()))
COLS_COLS = (((0,), (0,)), ((), ()))


def dot(a, b, dims):
    return lax.dot_general(a, b, dims, preferred_element_type=jnp.float32)


HEADS = [slice(h * HEAD_DIM, (h + 1) * HEAD_DIM) for h in range(2)]
STEPS = TOK // TILE


def band_kernel(own, *refs):
    if own:
        norm_ref, q_ref, g_ref, delta_ref, k_ref, v_ref, part_ref, dq_ref, dkv_ref = refs[:9]
    else:
        edge_ref, norm_ref, *refs = refs
        q_ref, g_ref, o_ref, k_ref, va_ref, *vb_refs = refs[:7]
        part_ref, dkv_ref, delta_ref, v_ref = refs[7:11]
    norm, dk_sum, dv_sum = refs[-3:]
    pair = pl.program_id(0)
    for h in range(2):
        row = norm_ref[pl.ds(pair * 2 + h, 1), :] * LOG2E
        if not own:
            row = row + edge_ref[0]
        norm[h] = jnp.broadcast_to(row, (8, TOK))

    if not own:
        for n, vb_ref in enumerate(vb_refs):
            at = slice(n * TOK // 2, (n + 1) * TOK // 2)
            v_ref[at, :] = va_ref[at, :] + vb_ref[...]
        ones = jnp.ones((8, HEAD_DIM), jnp.bfloat16)
        for h in range(2):
            terms = g_ref[:, HEADS[h]].astype(jnp.float32) * o_ref[:, HEADS[h]].astype(jnp.float32)
            high = terms.astype(jnp.bfloat16)
            low = (terms - high.astype(jnp.float32)).astype(jnp.bfloat16)
            total = dot(ones, high, ROWS_ROWS) + dot(ones, low, ROWS_ROWS)
            delta_ref[8 * h : 8 * h + 8, :] = total

    def tile(i, e, dq):
        at_q = slice(i * TILE, (i + 1) * TILE)
        at_k = slice(e * TILE, (e + 1) * TILE)
        k = k_ref[at_k, :]
        v = v_ref[at_k, :]
        if i == e:
            row = lax.broadcasted_iota(jnp.int32, (TILE, TILE), 0)
            col = lax.broadcasted_iota(jnp.int32, (TILE, TILE), 1)
            allowed = row <= col if own else row > col
        probs = []
        grads = []
        for h in range(2):
            scores = dot(k, q_ref[at_q, HEADS[h]], ROWS_ROWS)
            prob = jnp.exp2(scores * (SCALE * LOG2E) - norm[h, 0:1, at_q])
            if i == e:
                prob = jnp.where(allowed, prob, 0.0)
            grad_prob = dot(v, g_ref[at_q, HEADS[h]], ROWS_ROWS)
            delta = delta_ref[8 * h : 8 * h + 1, at_q]
            grads.append((prob * (grad_prob - delta)).astype(jnp.bfloat16))
            probs.append(prob.astype(jnp.bfloat16))
        dv = dot(probs[0], g_ref[at_q, HEADS[0]], ROWS_COLS) + dot(
            probs[1], g_ref[at_q, HEADS[1]], ROWS_COLS
        )
        dk = dot(grads[0], q_ref[at_q, HEADS[0]], ROWS_COLS) + dot(
            grads[1], q_ref[at_q, HEADS[1]], ROWS_COLS
        )
        if i == (e if own else 0):
            dv_sum[at_k, :] = dv
            dk_sum[at_k, :] = dk
        else:
            dv_sum[at_k, :] += dv
            dk_sum[at_k, :] += dk
        return [d + dot(k, grads[h], COLS_COLS) for h, d in enumerate(dq)]

    for i in range(STEPS):
        at_q = slice(i * TILE, (i + 1) * TILE)
        if own:
            dq = [part_ref[rows, at_q] for rows in HEADS]
        else:
            dq = [jnp.zeros((HEAD_DIM, TILE), jnp.float32)] * 2
        for e in range(0, i + 1) if own else range(i, STEPS):
            dq = tile(i, e, dq)
        for h in range(2):
            if own:
                dq_ref[at_q, HEADS[h]] = (dq[h] * SCALE).T.astype(jnp.bfloat16)
            else:
                part_ref[HEADS[h], at_q] = dq[h]
    kind = dkv_ref.dtype
    dkv_ref[:, 0:HEAD_DIM] = (dk_sum[...] * SCALE).astype(kind)
    dkv_ref[:, HEAD_DIM:] = dv_sum[...].astype(kind)


def band(own, *operands):
    spec = pl.BlockSpec
    wide = spec((TOK, PAIR), lambda i: (0, i))
    tall = spec((PAIR, TOK), lambda i: (i, 0))
    narrow = spec((TOK, HEAD_DIM), lambda i: (0, i))
    lines = spec((16, TOK), lambda i: (i, 0))
    shape = jax.ShapeDtypeStruct
    norm = spec((4, TOK), lambda i: (0, 0))
    scratch = [
        pltpu.VMEM((2, 8, TOK), jnp.float32),
        pltpu.VMEM((TOK, HEAD_DIM), jnp.float32),
        pltpu.VMEM((TOK, HEAD_DIM), jnp.float32),
    ]
    if own:
        in_specs = [norm, wide, wide, lines, narrow, narrow, tall]
        out_specs = [wide, wide]
        out_shape = [
            pltpu.HBM((TOK, 2 * PAIR), jnp.bfloat16),
            shape((TOK, 2 * PAIR), jnp.float32),
        ]
    else:
        half = spec((TOK // 2, HEAD_DIM), lambda i: (0, i))
        in_specs = [spec(memory_space=pltpu.SMEM), norm, wide, wide, wide, narrow, narrow, half, half]
        out_specs = [tall, wide, lines]
        out_shape = [
            shape((2 * PAIR, TOK), jnp.float32),
            shape((TOK, 2 * PAIR), jnp.bfloat16),
            shape((32, TOK), jnp.float32),
        ]
        scratch = [pltpu.VMEM((TOK, HEAD_DIM), jnp.bfloat16)] + scratch
    return pl.pallas_call(
        functools.partial(band_kernel, own),
        name="own_band" if own else "rim_band",
        grid=(2,),
        in_specs=in_specs,
        out_specs=out_specs,
        out_shape=out_shape,
        scratch_shapes=scratch,
        compiler_params=pltpu.CompilerParams(vmem_limit_bytes=20000 * 1024),
        cost_estimate=pl.CostEstimate(
            flops=4 * 10**9, bytes_accessed=8 * 2**20, transcendentals=3 * 10**6
        ),
    )(*operands)


def from_behind(shard, by, skip=None):
    devices = lax.axis_size("seq")
    pairs = [(i, i + by) for i in range(devices) if 0 <= i + by < devices and i != skip]
    return lax.ppermute(shard, "seq", pairs)


def prepare_kernel(g_ref, parts_ref, sem):
    members, _, width = parts_ref.shape
    copies = [
        pltpu.make_async_copy(g_ref.at[:, pl.ds(i * width, width)], parts_ref.at[i], sem.at[i])
        for i in range(members)
    ]
    for copy in copies:
        copy.start()
    for copy in copies:
        copy.wait()


def prepare(out_grad):
    members = lax.axis_size("head")
    rows, width = out_grad.shape
    shape = (members, rows, width // members)
    return pl.pallas_call(
        prepare_kernel,
        name="prepare",
        grid=(1,),
        in_specs=[pl.BlockSpec(memory_space=pl.ANY)],
        out_specs=pl.BlockSpec(shape, lambda i: (0, 0, 0)),
        out_shape=jax.ShapeDtypeStruct(shape, out_grad.dtype),
        scratch_shapes=[pltpu.SemaphoreType.DMA((members,))],
        compiler_params=pltpu.CompilerParams(vmem_limit_bytes=60 * 1024 * 1024),
        cost_estimate=pl.CostEstimate(flops=0, bytes_accessed=2 * 2**20, transcendentals=0),
    )(out_grad)


HOPS = [(0, 0), (1, 0), (2, 1), (0, 1), (3, 0), (1, 1), (2, 0), (3, 1)]


def sum_kernel(me_ref, own_ref, later_ref, *out_refs):
    rows = out_refs[0].shape[0]
    for hop, out_ref in zip(HOPS, out_refs):
        at = pl.ds(pl.multiple_of(partner(me_ref[0], hop) * rows, rows), rows)
        total = own_ref[at, :] + later_ref[at, :].astype(jnp.float32)
        out_ref[...] = total.astype(out_ref.dtype)


def sum_parts(me, own, later):
    members = lax.axis_size("head")
    rows = TOK // members
    vmem = pl.BlockSpec(memory_space=pltpu.VMEM)
    return pl.pallas_call(
        sum_kernel,
        name="sum_parts",
        in_specs=[pl.BlockSpec(memory_space=pltpu.SMEM), vmem, vmem],
        out_specs=[vmem] * members,
        out_shape=[jax.ShapeDtypeStruct((rows, 2 * PAIR), jnp.bfloat16)] * members,
        compiler_params=pltpu.CompilerParams(vmem_limit_bytes=6 * 2**20),
        cost_estimate=pl.CostEstimate(flops=10**6, bytes_accessed=4 * 2**20, transcendentals=0),
    )(me, own, later)


def join_kernel(me_ref, *refs):
    *in_refs, key_ref, value_ref = refs
    for shift, in_ref in enumerate(in_refs):
        source = partner(me_ref[0], (4 - HOPS[shift][0], HOPS[shift][1]))
        for g in range(2):
            to = pl.ds(pl.multiple_of(source * PAIR + g * HEAD_DIM, HEAD_DIM), HEAD_DIM)
            key_ref[:, to] = in_ref[:, g * PAIR : g * PAIR + HEAD_DIM]
            value_ref[:, to] = in_ref[:, g * PAIR + HEAD_DIM : (g + 1) * PAIR]


def join(me, parts):
    members = len(parts)
    rows = parts[0].shape[0]
    vmem = pl.BlockSpec(memory_space=pltpu.VMEM)
    out = jax.ShapeDtypeStruct((rows, members * PAIR), parts[0].dtype)
    return pl.pallas_call(
        join_kernel,
        name="join",
        grid=(1,),
        in_specs=[pl.BlockSpec(memory_space=pltpu.SMEM)]
        + [pl.BlockSpec(parts[0].shape, lambda i: (0, 0))] * members,
        out_specs=[pl.BlockSpec(out.shape, lambda i: (0, 0))] * 2,
        out_shape=[out, out],
        compiler_params=pltpu.CompilerParams(vmem_limit_bytes=16 * 2**20),
        cost_estimate=pl.CostEstimate(flops=0, bytes_accessed=4 * 2**20, transcendentals=0),
    )(me, *parts)


def exchange(parts):
    return lax.all_to_all(parts, "head", split_axis=0, concat_axis=0, tiled=True)


def partner(i, hop):
    z, half = hop
    return (i + 2 * z) % 8 ^ half


def shift_heads(x, hop):
    return lax.ppermute(x, "head", [(i, partner(i, hop)) for i in range(8)])


def on_device(queries, key_states, value_states, outputs, out_grad, log_norm):
    members = lax.axis_size("head")
    me = lax.axis_index("head").astype(jnp.int32).reshape(1)
    edge = jnp.where(lax.axis_index("seq") == 0, BIG, 0.0).astype(jnp.float32).reshape(1)
    half = lax.axis_size("seq") // 2
    middle = (1, half - 5)
    detours = []
    for n in range(2):
        rows = value_states[n * TOK // 2 : (n + 1) * TOK // 2]
        detours.append(lax.ppermute(rows, "seq", [(half - 1, middle[n])]))
    k_rim = from_behind(key_states, 1)
    v_rim = from_behind(value_states, 1, skip=half - 1)
    grad_parts = prepare(out_grad)
    grad_local = exchange(grad_parts).reshape(TOK, 2 * PAIR)
    v_far = []
    for n in range(2):
        v_far.append(lax.ppermute(detours[n], "seq", [(middle[n], half)]))
    queries_rim = pltpu.with_memory_space_constraint(queries, pltpu.HBM)
    part, rim, delta = band(
        False, edge, log_norm, queries_rim, grad_local, outputs, k_rim, v_rim, *v_far
    )
    later = from_behind(rim, -1)
    dq, own = band(True, log_norm, queries, grad_local, delta, key_states, value_states, part)
    dq = exchange(dq.reshape(members, TOK // members, 2 * PAIR))
    dkv = sum_parts(me, own, later)
    dkv = [dkv[0]] + [shift_heads(x, hop) for x, hop in zip(dkv[1:], HOPS[1:])]
    key_grad, value_grad = join(me, dkv)
    dq = dq.transpose(1, 0, 2).reshape(TOK // members, members * 2 * PAIR)
    return dq, key_grad, value_grad


def solution(mesh):
    placed = (
        P("seq", "head"),
        P("seq", "head"),
        P("seq", "head"),
        P("seq", "head"),
        P(("seq", "head"), None),
        P("head", "seq"),
    )
    return jax.shard_map(
        on_device,
        mesh=mesh,
        in_specs=placed,
        out_specs=(P(("seq", "head"), None), P(("seq", "head"), None), P(("seq", "head"), None)),
        check_vma=False,
    )
```
